32 devices in a mesh: sample: 2 (over core), outer: 2 (over y), inner: 8 (over z, x).
Axes of the slice: x: 2, y: 2, z: 4, core: 2. Of those that a mesh axis runs over, the one named last changes fastest.
Arguments:
- out_cotangent: bfloat16 [32, 384, 1152], P(('sample', 'outer', 'inner')), parts along dimension 0, may hold values from -6 to 6
- wo_spatial: bfloat16 [576, 1152], replicated, may hold values from -0.75 to 0.75
- wqkv_spatial: bfloat16 [1152, 1728], replicated, may hold values from -0.1875 to 0.1875
- wo_temporal: bfloat16 [576, 1152], replicated, may hold values from -0.75 to 0.75
- q_spatial: bfloat16 [32, 384, 576], P(('sample', 'outer', 'inner')), parts along dimension 0, may hold values from -6 to 6
- k_spatial: bfloat16 [32, 384, 576], P(('sample', 'outer', 'inner')), parts along dimension 0, may hold values from -6 to 6
- v_spatial: bfloat16 [32, 384, 576], P(('sample', 'outer', 'inner')), parts along dimension 0, may hold values from -6 to 6
- q_temporal: bfloat16 [32, 384, 576], P('sample', ('outer', 'inner')), parts along dimension 0, may hold values from -6 to 6
- k_temporal: bfloat16 [32, 384, 576], P('sample', ('outer', 'inner')), parts along dimension 0, may hold values from -6 to 6
- v_temporal: bfloat16 [32, 384, 576], P('sample', ('outer', 'inner')), parts along dimension 0, may hold values from -6 to 6
Outputs:
- middle_grad: bfloat16 [32, 384, 1152], P(('sample', 'outer', 'inner')), parts along dimension 0
- temporal_grads: bfloat16 [32, 384, 1728], P(('sample', 'outer', 'inner')), parts along dimension 0
The draws below stay inside these ranges and needn't reach their ends.
There are 2 independent parts, one for each index of `sample`. The reference program is written for one: setup_inputs(seed, part) draws one part's arguments, and reference() takes and returns one part's arrays. A program takes and returns all parts, laid end to end along the dimension named above; an argument that names none is the same for every part. Nothing has to cross between parts.
All inputs are finite; a program needn't handle non-finite values.
Results may differ from the reference program's by a relative error of at most 0.015.
Values may be sent and summed in bfloat16 or wider, within the bound.
No kernel may reach another device: no remote copies, remote signals or barrier semaphores. Data moves between devices by JAX's collectives and lax.ppermute only.
A program may use at most 64 MiB of HBM per device.

```python
import jax
import jax.numpy as jnp
from jax import lax

D = 1152
HEADS = 8
HEAD_DIM = 72
S = 384
FRAMES = 16


def drawn(key, salt):
    channels = HEADS * HEAD_DIM
    salted = jax.random.fold_in(key, salt)
    query_all = jnp.clip(jax.random.normal(jax.random.fold_in(salted, 1), (FRAMES, S, channels), jnp.float32), -4.5, 4.5)
    key_all = jnp.clip(jax.random.normal(jax.random.fold_in(salted, 2), (FRAMES, S, channels), jnp.float32), -4.5, 4.5)
    return (query_all, key_all)


def draw_q_spatial(key, part):
    return drawn(key, 11)[0].astype(jnp.bfloat16)


def draw_k_spatial(key, part):
    return drawn(key, 11)[1].astype(jnp.bfloat16)


def draw_q_temporal(key, part):
    return drawn(key, 23)[0].astype(jnp.bfloat16)


def draw_k_temporal(key, part):
    return drawn(key, 23)[1].astype(jnp.bfloat16)


def steps_of(stream_key, dims, shards, smallest, largest):
    def one(dim, shards_of):
        steps = jax.random.uniform(jax.random.fold_in(jax.random.fold_in(stream_key, 6), dim), (shards_of,), jnp.float32, smallest / len(shards), largest / len(shards))
        return jnp.repeat(jnp.exp(steps), dims[dim] // shards_of).reshape((-1,) + (1,) * (len(dims) - dim - 1))

    gain = one(*shards[0])
    for cut in shards[1:]:
        gain = gain * one(*cut)
    return gain


def noise(key, extent, spread, limit, shards=(), kind=jnp.bfloat16):
    array = spread * jax.random.normal(key, extent, jnp.float32)
    if shards:
        array = array * steps_of(key, extent, shards, -0.22, 0.18)
    return jnp.clip(array, -limit, limit).astype(kind)


def setup_inputs(seed: int = 0, part: int = 0) -> dict:
    seeds = jax.random.split(jax.random.key(seed), 11)
    part_splits = jax.random.split(jax.random.fold_in(seeds[10], part), 11)
    out_cotangent = noise(part_splits[0], (FRAMES, S, D), 1.0, 6.0, ((0, 16),))
    wo_spatial = noise(seeds[1], (HEADS * HEAD_DIM, D), HEAD_DIM ** -0.5, 0.75)
    wqkv_spatial = noise(seeds[2], (D, 3 * HEADS * HEAD_DIM), D ** -0.5, 0.1875)
    wo_temporal = noise(seeds[3], (HEADS * HEAD_DIM, D), HEAD_DIM ** -0.5, 0.75)
    q_spatial = draw_q_spatial(jax.random.fold_in(jax.random.fold_in(seeds[10], part), 71), part)
    k_spatial = draw_k_spatial(jax.random.fold_in(jax.random.fold_in(seeds[10], part), 71), part)
    v_spatial = noise(part_splits[6], (FRAMES, S, HEADS * HEAD_DIM), 1.0, 6.0, ((0, 16),))
    q_temporal = draw_q_temporal(jax.random.fold_in(jax.random.fold_in(seeds[10], part), 71), part)
    k_temporal = draw_k_temporal(jax.random.fold_in(jax.random.fold_in(seeds[10], part), 71), part)
    v_temporal = noise(part_splits[9], (FRAMES, S, HEADS * HEAD_DIM), 1.0, 6.0, ((1, 16),))
    return {"out_cotangent": out_cotangent, "wo_spatial": wo_spatial, "wqkv_spatial": wqkv_spatial, "wo_temporal": wo_temporal, "q_spatial": q_spatial, "k_spatial": k_spatial, "v_spatial": v_spatial, "q_temporal": q_temporal, "k_temporal": k_temporal, "v_temporal": v_temporal}


def attend_back(queries, key_rows, value_rows, grad_out):
    scaling = queries.shape[-1] ** -0.5
    q_full = queries.astype(jnp.float32)
    k_full = key_rows.astype(jnp.float32)
    v_full = value_rows.astype(jnp.float32)
    g_full = grad_out.astype(jnp.float32)
    scores = jnp.einsum('lbhe,mbhe->bhlm', q_full, k_full) * scaling
    row_max = jnp.max(scores, axis=-1, keepdims=True)
    weights = jnp.exp(scores - row_max)
    weights = weights / jnp.sum(weights, axis=-1, keepdims=True)
    weights_low = lax.optimization_barrier(weights.astype(jnp.bfloat16)).astype(jnp.float32)
    grad_value = jnp.einsum('bhlm,lbhe->mbhe', weights_low, g_full).astype(jnp.bfloat16)
    grad_weight = jnp.einsum('lbhe,mbhe->bhlm', g_full, v_full)
    row_inner = jnp.sum(weights * grad_weight, axis=-1, keepdims=True)
    grad_score = lax.optimization_barrier((weights * (grad_weight - row_inner)).astype(jnp.bfloat16)).astype(jnp.float32)
    grad_query = (jnp.einsum('bhlm,mbhe->lbhe', grad_score, k_full) * scaling).astype(jnp.bfloat16)
    grad_key = (jnp.einsum('bhlm,lbhe->mbhe', grad_score, q_full) * scaling).astype(jnp.bfloat16)
    return grad_query, grad_key, grad_value


def block_grads(items):
    queries, key_rows, value_rows, grad_out = items
    length = queries.shape[0]
    channels = queries.shape[1]
    shaped = [a.reshape(length, 1, HEADS, HEAD_DIM) for a in (queries, key_rows, value_rows, grad_out)]
    grad_query, grad_key, grad_value = attend_back(shaped[0], shaped[1], shaped[2], shaped[3])
    return jnp.concatenate([grad_query.reshape(length, channels), grad_key.reshape(length, channels), grad_value.reshape(length, channels)], axis=1)


def reference(out_cotangent, wo_spatial, wqkv_spatial, wo_temporal, q_spatial, k_spatial, v_spatial, q_temporal, k_temporal, v_temporal):
    channels = HEADS * HEAD_DIM
    grad_rows = out_cotangent.reshape(FRAMES * S, D)
    spatial_out = jnp.dot(grad_rows, wo_spatial.T, preferred_element_type=jnp.float32).astype(jnp.bfloat16)
    spatial_out = spatial_out.reshape(FRAMES, S, channels)
    spatial_grads = lax.map(block_grads, (q_spatial, k_spatial, v_spatial, spatial_out))
    spatial_term = jnp.dot(spatial_grads.reshape(FRAMES * S, 3 * channels), wqkv_spatial.T, preferred_element_type=jnp.float32)
    middle = (grad_rows.astype(jnp.float32) + spatial_term).astype(jnp.bfloat16)
    temporal_out = jnp.dot(middle, wo_temporal.T, preferred_element_type=jnp.float32).astype(jnp.bfloat16)
    temporal_out = temporal_out.reshape(FRAMES, S, channels)
    swapped = tuple(jnp.swapaxes(a, 0, 1) for a in (q_temporal, k_temporal, v_temporal, temporal_out))
    temporal_grads = jnp.swapaxes(lax.map(block_grads, swapped), 0, 1)
    return middle.reshape(FRAMES, S, D), temporal_grads
```

```python
import functools
import math

import jax
import jax.numpy as jnp
from jax import lax
from jax.experimental import pallas as pl
from jax.experimental.pallas import tpu as pltpu
from jax.sharding import PartitionSpec as P

HEADS = 8
F32 = jnp.float32
BF16 = jnp.bfloat16
NN = (((1,), (0,)), ((), ()))
NT = (((1,), (1,)), ((), ()))
TN = (((0,), (0,)), ((), ()))
LOG2E = math.log2(math.e)


def mm(a, b, dims):
    return lax.dot_general(a, b, dims, preferred_element_type=F32)


def spatial_kernel(
    cot_hbm, wos_hbm, wqkv_hbm, wot_hbm, q_hbm, k_hbm, v_hbm,
    mid_hbm, g_hbm,
    cot, wos, wqkv, wot, q, k, v, gs, sg, mid, g, sem,
):
    heads, dim, tokens = q.shape
    channels = heads * dim
    scaling = dim ** (-0.5)
    exp_scale = scaling * LOG2E
    loads = [
        pltpu.make_async_copy(src, dst, sem.at[i])
        for i, (src, dst) in enumerate(
            [(k_hbm, k), (q_hbm, q), (wos_hbm, wos), (cot_hbm, cot), (v_hbm, v),
             (wqkv_hbm, wqkv), (wot_hbm, wot)]
        )
    ]
    for copy in loads:
        copy.start()
    for copy in loads[:5]:
        copy.wait()
    gs[...] = mm(wos[...], cot[...], NT).reshape(heads, dim, tokens)
    for h in range(heads):
        q_t = q[h]
        k_t = k[h]
        keys = k_t.T
        scores = mm(keys, q_t, NN)
        top = jnp.max(scores, axis=0, keepdims=True)
        e = jnp.exp2((scores - top) * exp_scale)
        r = 1.0 / jnp.sum(e, axis=0, keepdims=True)
        e_low = e.astype(BF16)
        g_t = (gs[h] * r).astype(BF16)
        grad_w = mm(v[h].T, g_t, NN)
        inner = jnp.sum(e * grad_w, axis=0, keepdims=True) * r
        ds = (e * (grad_w - inner)).astype(BF16)
        dv = mm(g_t, e_low, NT)
        dk = mm(q_t, ds, NT) * scaling
        dq = mm(k_t, ds, NN) * scaling
        sg[h] = dq.astype(BF16)
        sg[heads + h] = dk.astype(BF16)
        sg[2 * heads + h] = dv.astype(BF16)
    loads[5].wait()
    grads = sg[...].reshape(3 * channels, tokens)
    middle = (cot[...].astype(F32) + mm(grads, wqkv[...], TN)).astype(BF16)
    mid[...] = middle
    out_mid = pltpu.make_async_copy(mid, mid_hbm, sem.at[7])
    out_mid.start()
    loads[6].wait()
    g[...] = mm(middle, wot[...], NT).astype(BF16)
    out_g = pltpu.make_async_copy(g, g_hbm, sem.at[8])
    out_g.start()
    out_mid.wait()
    out_g.wait()


def spatial(cot, wos, wqkv_t, wot, q_t, k_t, v_t):
    heads, dim, tokens = q_t.shape
    features = cot.shape[1]
    channels = heads * dim
    any_spec = pl.BlockSpec(memory_space=pl.ANY)
    hbm_spec = pl.BlockSpec(memory_space=pltpu.HBM)
    ins = [cot, wos, wqkv_t, wot, q_t, k_t, v_t]
    return pl.pallas_call(
        spatial_kernel,
        out_shape=(
            jax.ShapeDtypeStruct((tokens, features), BF16),
            jax.ShapeDtypeStruct((tokens, channels), BF16),
        ),
        in_specs=[hbm_spec] * 7,
        out_specs=(hbm_spec, any_spec),
        scratch_shapes=[pltpu.VMEM(a.shape, BF16) for a in ins]
        + [
            pltpu.VMEM((heads, dim, tokens), F32),
            pltpu.VMEM((3 * heads, dim, tokens), BF16),
            pltpu.VMEM((tokens, features), BF16),
            pltpu.VMEM((tokens, channels), BF16),
            pltpu.SemaphoreType.DMA((9,)),
        ],
        compiler_params=pltpu.CompilerParams(vmem_limit_bytes=66 * 1000 * 1000),
        name="spatial",
    )(*ins)


def temporal_kernel(q_ref, k_ref, v_ref, g_ref, o_ref):
    frames, positions, channels = q_ref.shape
    dim = channels // HEADS
    scaling = dim ** (-0.5)
    exp_scale = scaling * LOG2E
    step = math.gcd(positions, 8)
    rows = frames * step
    row = lax.broadcasted_iota(jnp.int32, (rows, rows), 0)
    col = lax.broadcasted_iota(jnp.int32, (rows, rows), 1)
    bias = jnp.where(lax.rem(row, step) == lax.rem(col, step), 0.0, -1e30).astype(F32)
    for j in range(positions // step):
        at = pl.ds(j * step, step)

        def load(ref):
            return ref[:, at, :].astype(F32).reshape(rows, channels).astype(BF16)

        q, k, v, g = load(q_ref), load(k_ref), load(v_ref), load(g_ref)
        parts = [[], [], []]
        for h in range(HEADS):
            cut = slice(h * dim, (h + 1) * dim)
            q_h, k_h, v_h, g_h = q[:, cut], k[:, cut], v[:, cut], g[:, cut]
            scores = mm(k_h, q_h, NT) + bias
            top = jnp.max(scores, axis=0, keepdims=True)
            e = jnp.exp2((scores - top) * exp_scale)
            p = e * (1.0 / jnp.sum(e, axis=0, keepdims=True))
            grad_w = mm(v_h, g_h, NT)
            inner = jnp.sum(p * grad_w, axis=0, keepdims=True)
            ds = (p * (grad_w - inner)).astype(BF16)
            parts[0].append(mm(ds, k_h, TN) * scaling)
            parts[1].append(mm(ds, q_h, NN) * scaling)
            parts[2].append(mm(p.astype(BF16), g_h, NN))
        whole = jnp.concatenate(parts[0] + parts[1] + parts[2], axis=1)
        o_ref[:, at, :] = whole.reshape(frames, step, 3 * channels).astype(BF16)


def temporal(q, k, v, g):
    frames, positions, channels = q.shape
    return pl.pallas_call(
        temporal_kernel,
        out_shape=jax.ShapeDtypeStruct((frames, positions, 3 * channels), BF16),
        compiler_params=pltpu.CompilerParams(vmem_limit_bytes=32 << 20),
        name="temporal",
    )(q, k, v, g)


def local(cot, wos, wqkv, wot, qs, ks, vs, qt, kt, vt):
    tokens, features = cot.shape[1:]
    channels = qs.shape[2]
    dim = channels // HEADS
    axes = ("outer", "inner")
    groups = lax.axis_size(axes)
    pos_dev = tokens // groups

    def by_head(a):
        return a[0].T.reshape(HEADS, dim, tokens)

    middle, projected = spatial(
        cot[0], wos, wqkv.T, wot, by_head(qs), by_head(ks), by_head(vs)
    )
    temporal_out = lax.all_to_all(
        projected.reshape(groups, pos_dev, channels), axes, split_axis=0, concat_axis=0, tiled=True
    )
    stacked = temporal(qt, kt, vt, temporal_out)
    returned = lax.all_to_all(stacked, axes, split_axis=0, concat_axis=0, tiled=True)
    return (middle[None], returned.reshape(1, tokens, 3 * channels))


def solution(mesh):
    frame = P(("sample", "outer", "inner"), None, None)
    place = P("sample", ("outer", "inner"), None)
    return jax.shard_map(
        local,
        mesh=mesh,
        in_specs=(frame, P(), P(), P(), frame, frame, frame, place, place, place),
        out_specs=(frame, frame),
        check_vma=False,
    )
```

```python
import functools
import math

import jax
import jax.numpy as jnp
from jax import lax
from jax.experimental import pallas as pl
from jax.experimental.pallas import tpu as pltpu
from jax.sharding import PartitionSpec as P

HEADS = 8
F32 = jnp.float32
BF16 = jnp.bfloat16
NN = (((1,), (0,)), ((), ()))
NT = (((1,), (1,)), ((), ()))
TN = (((0,), (0,)), ((), ()))
LANES = 128
LOG2E = math.log2(math.e)


def mm(a, b, dims):
    return lax.dot_general(a, b, dims, preferred_element_type=F32)


def pair_windows(channels, dim):
    found = []
    for h in range(0, HEADS, 2):
        low = h * dim // LANES * LANES
        high = min(channels, -(-(h + 2) * dim // LANES) * LANES)
        found.append((h, low, high))
    return found


def stack_pair(block, h, low, dim):
    lane = low + lax.broadcasted_iota(jnp.int32, block.shape, 1)
    zero = jnp.zeros_like(block)
    first = (lane >= h * dim) & (lane < (h + 1) * dim)
    second = (lane >= (h + 1) * dim) & (lane < (h + 2) * dim)
    return jnp.concatenate([jnp.where(first, block, zero), jnp.where(second, block, zero)], axis=0)


def softmax_rows(scores, exp_scale):
    top = jnp.max(scores, axis=0, keepdims=True)
    e = jnp.exp2((scores - top) * exp_scale)
    return e * (1.0 / jnp.sum(e, axis=0, keepdims=True))


def score_grad(p, grad_w):
    inner = jnp.sum(p * grad_w, axis=0, keepdims=True)
    return (p * (grad_w - inner)).astype(BF16)


def turn_halves(ds, rows):
    return jnp.concatenate([ds[:, :rows].T, ds[:, rows:].T], axis=1)


def add_tiles(tiles, window, low):
    for t in range(0, window.shape[1], LANES):
        piece = window[:, t : t + LANES]
        tiles[low + t] = tiles[low + t] + piece if low + t in tiles else piece


def spatial_kernel(
    cot_hbm, wos_hbm, wqkv_hbm, wot_hbm, q_hbm, k_hbm, v_hbm,
    mid_hbm, g,
    cot, wos, wqkv, wot, q, k, v, probs, sg, mid, sem,
):
    channels, tokens = q.shape
    dim = channels // HEADS
    scaling = dim ** (-0.5)
    exp_scale = scaling * LOG2E
    tail = channels % LANES
    body = channels - tail
    pairs = [(k_hbm, k), (q_hbm, q), (cot_hbm, cot), (wos_hbm, wos), (v_hbm, v), (wot_hbm, wot)]
    for n in range(3):
        pairs.append((wqkv_hbm.at[pl.ds(n * channels, body)], wqkv.at[pl.ds(n * body, body)]))
    if tail:
        for n in range(3):
            pairs.append(
                (wqkv_hbm.at[pl.ds(n * channels + body, tail)], wqkv.at[pl.ds(3 * body + n * tail, tail)])
            )
    loads = [pltpu.make_async_copy(src, dst, sem.at[i]) for i, (src, dst) in enumerate(pairs)]
    for copy in loads[:5]:
        copy.start()
    windows = pair_windows(channels, dim)
    for copy in loads[:2]:
        copy.wait()
    for copy in loads[5:]:
        copy.start()
    k_n = k[...].T
    q_n = q[...].T

    def scores_of(n):
        h, low, high = windows[n]
        return mm(k_n[:, low:high], stack_pair(q_n[:, low:high], h, low, dim), NT)

    count = len(windows)
    scores = [scores_of(0), scores_of(1)]
    probs[0] = softmax_rows(scores[0], exp_scale)
    for copy in loads[2:5]:
        copy.wait()
    g_n = mm(cot[...], wos[...], NT).astype(BF16)
    probs[1] = softmax_rows(scores[1], exp_scale)
    v_n = v[...].T

    def grad_of(n):
        h, low, high = windows[n]
        stack = stack_pair(g_n[:, low:high], h, low, dim)
        return stack, mm(v_n[:, low:high], stack, NT)

    tiles = [{}, {}, {}]
    ahead = grad_of(0)
    for n, (h, low, high) in enumerate(windows):
        g_s, grad_w = ahead
        p = probs[n]
        if n + 1 < count:
            ahead = grad_of(n + 1)
        add_tiles(tiles[2], mm(p.astype(BF16), g_s, NN), low)
        if n + 2 < count:
            scores.append(scores_of(n + 2))
        ds = score_grad(p, grad_w)
        if n + 2 < count:
            probs[n + 2] = softmax_rows(scores[n + 2], exp_scale)
        add_tiles(tiles[1], mm(ds, stack_pair(q_n[:, low:high], h, low, dim), NN), low)
        add_tiles(tiles[0], mm(turn_halves(ds, tokens), stack_pair(k_n[:, low:high], h, low, dim), NN), low)
    for n in range(3):
        for t, tile in sorted(tiles[n].items()):
            if n < 2:
                tile = tile * scaling
            width = tile.shape[1]
            at = n * body + t if t < body else 3 * body + n * tail + t - body
            sg[:, at : at + width] = tile.astype(BF16)
    for copy in loads[6:]:
        copy.wait()
    middle = (cot[...].astype(F32) + mm(sg[...], wqkv[...], NN)).astype(BF16)
    mid[...] = middle
    out_mid = pltpu.make_async_copy(mid, mid_hbm, sem.at[len(loads)])
    out_mid.start()
    loads[5].wait()
    g[...] = mm(middle, wot[...], NT).astype(BF16)
    out_mid.wait()


def spatial(cot, wos, wqkv_t, wot, q_t, k_t, v_t):
    channels, tokens = q_t.shape
    features = cot.shape[1]
    hbm_spec = pl.BlockSpec(memory_space=pltpu.HBM)
    ins = [cot, wos, wqkv_t, wot, q_t, k_t, v_t]
    ins = [pltpu.with_memory_space_constraint(a, pltpu.HBM) for a in ins]
    return pl.pallas_call(
        spatial_kernel,
        out_shape=(
            jax.ShapeDtypeStruct((tokens, features), BF16),
            pltpu.VMEM((tokens, channels), BF16),
        ),
        in_specs=[hbm_spec] * 7,
        out_specs=(hbm_spec, pl.BlockSpec(memory_space=pltpu.VMEM)),
        scratch_shapes=[pltpu.VMEM(a.shape, BF16) for a in ins]
        + [
            pltpu.VMEM((HEADS // 2, tokens, 2 * tokens), F32),
            pltpu.VMEM((tokens, 3 * channels), BF16),
            pltpu.VMEM((tokens, features), BF16),
            pltpu.SemaphoreType.DMA((13,)),
        ],
        compiler_params=pltpu.CompilerParams(vmem_limit_bytes=40 << 20),
        name="spatial",
    )(*ins)


def partner_of(s):
    return (lax.axis_index("outer") * lax.axis_size("inner") + lax.axis_index("inner")) ^ s


def frame_rows(ref, order, at, split):
    frames, _, channels = ref.shape
    if split:
        rows = [ref[partner_of(s), at, :].astype(F32) for s in order]
        block = jnp.concatenate(rows, axis=0)
    else:
        block = ref[:, at, :].astype(F32).reshape(-1, channels)
    return block.astype(BF16)


def probs_kernel(split, order, q_ref, k_ref, p_ref):
    frames, positions, channels = q_ref.shape
    dim = channels // HEADS
    exp_scale = dim ** (-0.5) * LOG2E
    step = math.gcd(positions, 8)
    rows = frames * step
    row = lax.broadcasted_iota(jnp.int32, (rows, 2 * rows), 0)
    col = lax.broadcasted_iota(jnp.int32, (rows, 2 * rows), 1)
    bias = jnp.where(lax.rem(row, step) == lax.rem(col, step), 0.0, -1e30).astype(F32)
    for j in range(positions // step):
        at = pl.ds(j * step, step)
        q, k = (frame_rows(a, order, at, split) for a in (q_ref, k_ref))
        for n, (h, low, high) in enumerate(pair_windows(channels, dim)):
            scores = mm(k[:, low:high], stack_pair(q[:, low:high], h, low, dim), NT)
            p_ref[j, n] = softmax_rows(scores + bias, exp_scale)


def probs(order, q, k, split):
    frames, positions, channels = q.shape
    step = math.gcd(positions, 8)
    rows = frames * step
    blocks = positions // step
    return pl.pallas_call(
        functools.partial(probs_kernel, split, order),
        out_shape=jax.ShapeDtypeStruct((blocks, HEADS // 2, rows, 2 * rows), F32),
        in_specs=[pl.BlockSpec(memory_space=pltpu.VMEM)] * 2,
        out_specs=pl.BlockSpec(memory_space=pltpu.VMEM),
        compiler_params=pltpu.CompilerParams(vmem_limit_bytes=24 << 20),
        cost_estimate=pl.CostEstimate(
            flops=blocks * HEADS * rows * rows * 1024,
            bytes_accessed=blocks * HEADS * rows * rows * 16,
            transcendentals=blocks * HEADS * rows * rows,
        ),
        name="probs",
    )(q, k)


def temporal_kernel(order, q_ref, k_ref, v_ref, p_ref, g_ref, *o_refs):
    frames, positions, channels = q_ref.shape
    dim = channels // HEADS
    scaling = dim ** (-0.5)
    step = math.gcd(positions, 8)
    rows = frames * step
    tail = channels % LANES
    split = len(o_refs) > 1
    windows = pair_windows(channels, dim)
    blocks = [pl.ds(j * step, step) for j in range(positions // step)]

    def begin(at):
        v, g = (frame_rows(a, order, at, split) for a in (v_ref, g_ref))
        stacks = [stack_pair(g[:, low:high], h, low, dim) for h, low, high in windows]
        return stacks, [mm(v[:, w[1] : w[2]], g_s, NT) for w, g_s in zip(windows, stacks)]

    ahead = begin(blocks[0])
    for j, at in enumerate(blocks):
        g_stacks, grads = ahead
        q, k = (frame_rows(a, order, at, split) for a in (q_ref, k_ref))
        if j + 1 < len(blocks):
            ahead = begin(blocks[j + 1])
        scores = [score_grad(p_ref[j, n], grad_w) for n, grad_w in enumerate(grads)]
        flipped = [turn_halves(ds, rows) for ds in scores]
        tiles = [{}, {}, {}]
        for n, (h, low, high) in enumerate(windows):
            q_s, k_s = (stack_pair(a[:, low:high], h, low, dim) for a in (q, k))
            add_tiles(tiles[2], mm(p_ref[j, n].astype(BF16), g_stacks[n], NN), low)
            add_tiles(tiles[1], mm(scores[n], q_s, NN), low)
            add_tiles(tiles[0], mm(flipped[n], k_s, NN), low)
        pieces, tails = [], []
        for n in range(3):
            part = [tile * scaling if n < 2 else tile for _, tile in sorted(tiles[n].items())]
            if tail:
                tails.append(part.pop())
            pieces += part
        whole = jnp.concatenate(pieces + tails, axis=1)
        if split:
            for s in range(frames):
                o_refs[s][at, :] = whole[s * step : (s + 1) * step].astype(BF16)
        else:
            o_refs[0][:, at, :] = whole.reshape(frames, step, 3 * channels).astype(BF16)


def temporal(order, q, k, v, p, g, split):
    frames, positions, channels = q.shape
    if split:
        shapes = [jax.ShapeDtypeStruct((positions, 3 * channels), BF16)] * frames
    else:
        shapes = [jax.ShapeDtypeStruct((frames, positions, 3 * channels), BF16)]
    return pl.pallas_call(
        functools.partial(temporal_kernel, order),
        out_shape=shapes,
        in_specs=[pl.BlockSpec(memory_space=pltpu.VMEM)] * 5,
        out_specs=[pl.BlockSpec(memory_space=pltpu.VMEM)] * len(shapes),
        compiler_params=pltpu.CompilerParams(vmem_limit_bytes=24 << 20),
        name="temporal",
    )(q, k, v, p, g)


def place_blocks(order, blocks, whole):
    for s, block in zip(order, blocks):
        each = block.shape[0]
        row = pl.multiple_of(partner_of(s) * each, 8)
        whole[pl.ds(row, each), :] = block[...]


def stage_kernel(order, *refs):
    place_blocks(order, refs[:-1], refs[-1])


def stage(order, blocks, tokens):
    width = blocks[0].shape[1]
    return pl.pallas_call(
        functools.partial(stage_kernel, order),
        out_shape=pltpu.VMEM((tokens, width), BF16),
        in_specs=[pl.BlockSpec(memory_space=pltpu.VMEM)] * len(blocks),
        out_specs=pl.BlockSpec(memory_space=pltpu.VMEM),
        compiler_params=pltpu.CompilerParams(vmem_limit_bytes=16 << 20),
        name="stage",
    )(*blocks)


def turn_kernel(order, staged, *refs):
    blocks, whole, o_hbm, turned, sem = refs[:-4], refs[-4], refs[-3], refs[-2], refs[-1]
    width = whole.shape[1]
    channels = width // 3
    tail = channels % LANES
    body = channels - tail
    place_blocks(order, blocks, whole)
    spans = [(n * body, n * channels, body) for n in range(3)]
    if tail:
        spans += [(3 * body + n * tail, n * channels + body, tail) for n in range(3)]
    stores = []
    for i, (source, target, size) in enumerate(spans):
        turned[pl.ds(target, size), :] = whole[:, pl.ds(source, size)].T
        rows = pl.ds(target, size)
        stores.append(pltpu.make_async_copy(turned.at[rows], o_hbm.at[rows], sem.at[i]))
        stores[-1].start()
    for copy in stores:
        copy.wait()


def turn(order, staged, blocks):
    tokens, width = staged.shape
    return pl.pallas_call(
        functools.partial(turn_kernel, order),
        out_shape=(
            pltpu.VMEM((tokens, width), BF16),
            jax.ShapeDtypeStruct((width, tokens), BF16),
        ),
        in_specs=[pl.BlockSpec(memory_space=pltpu.VMEM)] * (1 + len(blocks)),
        out_specs=[pl.BlockSpec(memory_space=pltpu.VMEM), pl.BlockSpec(memory_space=pltpu.HBM)],
        scratch_shapes=[pltpu.VMEM((width, tokens), BF16), pltpu.SemaphoreType.DMA((6,))],
        input_output_aliases={0: 0},
        compiler_params=pltpu.CompilerParams(vmem_limit_bytes=24 << 20),
        name="turn",
    )(staged, *blocks)[1]


def partner_order(groups, inner):
    by_hops = sorted(range(1, groups), key=lambda s: (bin(s).count("1"), s))
    across = [s for s in by_hops if s % inner >= inner // 2]
    beside = [s for s in by_hops if s % inner < inner // 2]
    found = []
    while across or beside:
        found += across[:1] + beside[:1]
        across, beside = across[1:], beside[1:]
    return found


def local(cot, wos, wqkv, wot, qs, ks, vs, qt, kt, vt):
    tokens, features = cot.shape[1:]
    channels = qs.shape[2]
    axes = ("outer", "inner")
    groups = lax.axis_size(axes)
    pos_dev = tokens // groups
    direct = groups <= 16 and groups & (groups - 1) == 0 and pos_dev % 8 == 0
    partners = [0] + partner_order(groups, lax.axis_size("inner")) if direct else []

    middle, projected = spatial(
        cot[0], wos, wqkv.T, wot, qs[0].T, ks[0].T, vs[0].T
    )
    temporal_out = lax.all_to_all(
        projected.reshape(groups, pos_dev, channels), axes, split_axis=0, concat_axis=0, tiled=True
    )
    weights = probs(partners, qt, kt, direct)
    stacked = temporal(partners, qt, kt, vt, weights, temporal_out, direct)
    if direct:
        blocks = list(stacked)
        for n, s in enumerate(partners):
            if s:
                blocks[n] = lax.ppermute(stacked[n], axes, [(i, i ^ s) for i in range(groups)])
    else:
        returned = lax.all_to_all(stacked[0], axes, split_axis=0, concat_axis=0, tiled=True)
        blocks = [returned.reshape(tokens, 3 * channels)]
    late = len(blocks) * 5 // 16
    early = len(blocks) - late
    staged = stage(partners[:early], blocks[:early], tokens) if late else blocks[0]
    turned = turn(partners[early:], staged, blocks[early:])
    return (middle[None], turned.T[None])


def solution(mesh):
    frame = P(("sample", "outer", "inner"), None, None)
    place = P("sample", ("outer", "inner"), None)
    return jax.shard_map(
        local,
        mesh=mesh,
        in_specs=(frame, P(), P(), P(), frame, frame, frame, place, place, place),
        out_specs=(frame, frame),
        check_vma=False,
    )
```

```python
import functools
import math

import jax
import jax.numpy as jnp
from jax import lax
from jax.experimental import pallas as pl
from jax.experimental.pallas import tpu as pltpu
from jax.sharding import PartitionSpec as P

HEADS = 8
F32 = jnp.float32
BF16 = jnp.bfloat16
NN = (((1,), (0,)), ((), ()))
NT = (((1,), (1,)), ((), ()))
TN = (((0,), (0,)), ((), ()))
LANES = 128
LOG2E = math.log2(math.e)


def mm(a, b, dims):
    return lax.dot_general(a, b, dims, preferred_element_type=F32)


def pair_windows(channels, dim):
    found = []
    for h in range(0, HEADS, 2):
        low = h * dim // LANES * LANES
        high = min(channels, -(-(h + 2) * dim // LANES) * LANES)
        found.append((h, low, high))
    return found


def stack_pair(block, h, low, dim):
    lane = low + lax.broadcasted_iota(jnp.int32, block.shape, 1)
    zero = jnp.zeros_like(block)
    first = (lane >= h * dim) & (lane < (h + 1) * dim)
    second = (lane >= (h + 1) * dim) & (lane < (h + 2) * dim)
    return jnp.concatenate([jnp.where(first, block, zero), jnp.where(second, block, zero)], axis=0)


def softmax_rows(scores, exp_scale):
    top = jnp.max(scores, axis=0, keepdims=True)
    e = jnp.exp2((scores - top) * exp_scale)
    return e * (1.0 / jnp.sum(e, axis=0, keepdims=True))


def score_grad(p, grad_w):
    inner = jnp.sum(p * grad_w, axis=0, keepdims=True)
    return (p * (grad_w - inner)).astype(BF16)


def turn_halves(ds, rows):
    return jnp.concatenate([ds[:, :rows].T, ds[:, rows:].T], axis=1)


def add_tiles(tiles, window, low):
    for t in range(0, window.shape[1], LANES):
        piece = window[:, t : t + LANES]
        tiles[low + t] = tiles[low + t] + piece if low + t in tiles else piece


def spatial_kernel(
    cot_hbm, wos_hbm, wqkv_hbm, wot_hbm, q_hbm, k_hbm, v_hbm,
    mid_hbm, g,
    cot, wos, wqkv, wot, q, k, v, probs, sg, mid, sem,
):
    channels, tokens = q.shape
    dim = channels // HEADS
    scaling = dim ** (-0.5)
    exp_scale = scaling * LOG2E
    tail = channels % LANES
    body = channels - tail
    pairs = [(k_hbm, k), (q_hbm, q), (cot_hbm, cot), (wos_hbm, wos), (v_hbm, v), (wot_hbm, wot)]
    for n in range(3):
        pairs.append((wqkv_hbm.at[pl.ds(n * channels, body)], wqkv.at[pl.ds(n * body, body)]))
    if tail:
        for n in range(3):
            pairs.append(
                (wqkv_hbm.at[pl.ds(n * channels + body, tail)], wqkv.at[pl.ds(3 * body + n * tail, tail)])
            )
    loads = [pltpu.make_async_copy(src, dst, sem.at[i]) for i, (src, dst) in enumerate(pairs)]
    for copy in loads[:5]:
        copy.start()
    windows = pair_windows(channels, dim)
    for copy in loads[:2]:
        copy.wait()
    for copy in loads[5:]:
        copy.start()
    k_n = k[...].T
    q_n = q[...].T

    def scores_of(n):
        h, low, high = windows[n]
        return mm(k_n[:, low:high], stack_pair(q_n[:, low:high], h, low, dim), NT)

    count = len(windows)
    scores = [scores_of(0), scores_of(1)]
    probs[0] = softmax_rows(scores[0], exp_scale)
    for copy in loads[2:5]:
        copy.wait()
    g_n = mm(cot[...], wos[...], NT).astype(BF16)
    probs[1] = softmax_rows(scores[1], exp_scale)
    v_n = v[...].T

    def grad_of(n):
        h, low, high = windows[n]
        stack = stack_pair(g_n[:, low:high], h, low, dim)
        return stack, mm(v_n[:, low:high], stack, NT)

    tiles = [{}, {}, {}]
    ahead = grad_of(0)
    for n, (h, low, high) in enumerate(windows):
        g_s, grad_w = ahead
        p = probs[n]
        if n + 1 < count:
            ahead = grad_of(n + 1)
        add_tiles(tiles[2], mm(p.astype(BF16), g_s, NN), low)
        if n + 2 < count:
            scores.append(scores_of(n + 2))
        ds = score_grad(p, grad_w)
        if n + 2 < count:
            probs[n + 2] = softmax_rows(scores[n + 2], exp_scale)
        add_tiles(tiles[1], mm(ds, stack_pair(q_n[:, low:high], h, low, dim), NN), low)
        add_tiles(tiles[0], mm(turn_halves(ds, tokens), stack_pair(k_n[:, low:high], h, low, dim), NN), low)
    for n in range(3):
        for t, tile in sorted(tiles[n].items()):
            if n < 2:
                tile = tile * scaling
            width = tile.shape[1]
            at = n * body + t if t < body else 3 * body + n * tail + t - body
            sg[:, at : at + width] = tile.astype(BF16)
    for copy in loads[6:]:
        copy.wait()
    middle = (cot[...].astype(F32) + mm(sg[...], wqkv[...], NN)).astype(BF16)
    mid[...] = middle
    out_mid = pltpu.make_async_copy(mid, mid_hbm, sem.at[len(loads)])
    out_mid.start()
    loads[5].wait()
    g[...] = mm(middle, wot[...], NT).astype(BF16)
    out_mid.wait()


def spatial(cot, wos, wqkv_t, wot, q_t, k_t, v_t):
    channels, tokens = q_t.shape
    features = cot.shape[1]
    hbm_spec = pl.BlockSpec(memory_space=pltpu.HBM)
    ins = [cot, wos, wqkv_t, wot, q_t, k_t, v_t]
    ins = [pltpu.with_memory_space_constraint(a, pltpu.HBM) for a in ins]
    return pl.pallas_call(
        spatial_kernel,
        out_shape=(
            jax.ShapeDtypeStruct((tokens, features), BF16),
            pltpu.VMEM((tokens, channels), BF16),
        ),
        in_specs=[hbm_spec] * 7,
        out_specs=(hbm_spec, pl.BlockSpec(memory_space=pltpu.VMEM)),
        scratch_shapes=[pltpu.VMEM(a.shape, BF16) for a in ins]
        + [
            pltpu.VMEM((HEADS // 2, tokens, 2 * tokens), F32),
            pltpu.VMEM((tokens, 3 * channels), BF16),
            pltpu.VMEM((tokens, features), BF16),
            pltpu.SemaphoreType.DMA((13,)),
        ],
        compiler_params=pltpu.CompilerParams(vmem_limit_bytes=40 << 20),
        name="spatial",
    )(*ins)


def partner_of(s):
    return (lax.axis_index("outer") * lax.axis_size("inner") + lax.axis_index("inner")) ^ s


def frame_rows(ref, order, at, split):
    frames, _, channels = ref.shape
    if split:
        rows = [ref[partner_of(s), at, :].astype(F32) for s in order]
        block = jnp.concatenate(rows, axis=0)
    else:
        block = ref[:, at, :].astype(F32).reshape(-1, channels)
    return block.astype(BF16)


def probs_kernel(split, order, q_ref, k_ref, p_ref):
    frames, positions, channels = q_ref.shape
    dim = channels // HEADS
    exp_scale = dim ** (-0.5) * LOG2E
    step = math.gcd(positions, 8)
    rows = frames * step
    row = lax.broadcasted_iota(jnp.int32, (rows, 2 * rows), 0)
    col = lax.broadcasted_iota(jnp.int32, (rows, 2 * rows), 1)
    bias = jnp.where(lax.rem(row, step) == lax.rem(col, step), 0.0, -1e30).astype(F32)
    for j in range(positions // step):
        at = pl.ds(j * step, step)
        q, k = (frame_rows(a, order, at, split) for a in (q_ref, k_ref))
        for n, (h, low, high) in enumerate(pair_windows(channels, dim)):
            scores = mm(k[:, low:high], stack_pair(q[:, low:high], h, low, dim), NT)
            p_ref[j, n] = softmax_rows(scores + bias, exp_scale)


def probs(order, q, k, split):
    frames, positions, channels = q.shape
    step = math.gcd(positions, 8)
    rows = frames * step
    blocks = positions // step
    return pl.pallas_call(
        functools.partial(probs_kernel, split, order),
        out_shape=jax.ShapeDtypeStruct((blocks, HEADS // 2, rows, 2 * rows), F32),
        in_specs=[pl.BlockSpec(memory_space=pltpu.VMEM)] * 2,
        out_specs=pl.BlockSpec(memory_space=pltpu.VMEM),
        compiler_params=pltpu.CompilerParams(vmem_limit_bytes=24 << 20),
        cost_estimate=pl.CostEstimate(
            flops=blocks * HEADS * rows * rows * 1024,
            bytes_accessed=blocks * HEADS * rows * rows * 16,
            transcendentals=blocks * HEADS * rows * rows,
        ),
        name="probs",
    )(q, k)


def temporal_kernel(order, q_ref, k_ref, v_ref, p_ref, g_ref, *o_refs):
    frames, positions, channels = q_ref.shape
    dim = channels // HEADS
    scaling = dim ** (-0.5)
    step = math.gcd(positions, 8)
    rows = frames * step
    tail = channels % LANES
    split = len(o_refs) > 1
    windows = pair_windows(channels, dim)
    blocks = [pl.ds(j * step, step) for j in range(positions // step)]

    def begin(at):
        v, g = (frame_rows(a, order, at, split) for a in (v_ref, g_ref))
        stacks = [stack_pair(g[:, low:high], h, low, dim) for h, low, high in windows]
        return stacks, [mm(v[:, w[1] : w[2]], g_s, NT) for w, g_s in zip(windows, stacks)]

    ahead = begin(blocks[0])
    for j, at in enumerate(blocks):
        g_stacks, grads = ahead
        q, k = (frame_rows(a, order, at, split) for a in (q_ref, k_ref))
        if j + 1 < len(blocks):
            ahead = begin(blocks[j + 1])
        scores = [score_grad(p_ref[j, n], grad_w) for n, grad_w in enumerate(grads)]
        flipped = [turn_halves(ds, rows) for ds in scores]
        tiles = [{}, {}, {}]
        for n, (h, low, high) in enumerate(windows):
            q_s, k_s = (stack_pair(a[:, low:high], h, low, dim) for a in (q, k))
            add_tiles(tiles[2], mm(p_ref[j, n].astype(BF16), g_stacks[n], NN), low)
            add_tiles(tiles[1], mm(scores[n], q_s, NN), low)
            add_tiles(tiles[0], mm(flipped[n], k_s, NN), low)
        pieces, tails = [], []
        for n in range(3):
            part = [tile * scaling if n < 2 else tile for _, tile in sorted(tiles[n].items())]
            if tail:
                tails.append(part.pop())
            pieces += part
        whole = jnp.concatenate(pieces + tails, axis=1)
        if split:
            for s in range(frames):
                o_refs[s][at, :] = whole[s * step : (s + 1) * step].astype(BF16)
        else:
            o_refs[0][:, at, :] = whole.reshape(frames, step, 3 * channels).astype(BF16)


def temporal(order, q, k, v, p, g, split):
    frames, positions, channels = q.shape
    if split:
        shapes = [jax.ShapeDtypeStruct((positions, 3 * channels), BF16)] * frames
    else:
        shapes = [jax.ShapeDtypeStruct((frames, positions, 3 * channels), BF16)]
    return pl.pallas_call(
        functools.partial(temporal_kernel, order),
        out_shape=shapes,
        in_specs=[pl.BlockSpec(memory_space=pltpu.VMEM)] * 5,
        out_specs=[pl.BlockSpec(memory_space=pltpu.VMEM)] * len(shapes),
        compiler_params=pltpu.CompilerParams(vmem_limit_bytes=24 << 20),
        name="temporal",
    )(q, k, v, p, g)


def place_blocks(order, blocks, whole):
    for s, block in zip(order, blocks):
        each = block.shape[0]
        row = pl.multiple_of(partner_of(s) * each, 8)
        whole[pl.ds(row, each), :] = block[...]


def stage_kernel(order, *refs):
    place_blocks(order, refs[:-1], refs[-1])


def stage(order, blocks, tokens):
    width = blocks[0].shape[1]
    return pl.pallas_call(
        functools.partial(stage_kernel, order),
        out_shape=pltpu.VMEM((tokens, width), BF16),
        in_specs=[pl.BlockSpec(memory_space=pltpu.VMEM)] * len(blocks),
        out_specs=pl.BlockSpec(memory_space=pltpu.VMEM),
        compiler_params=pltpu.CompilerParams(vmem_limit_bytes=16 << 20),
        name="stage",
    )(*blocks)


def turn_kernel(order, staged, *refs):
    blocks, whole, o_hbm, turned, sem = refs[:-4], refs[-4], refs[-3], refs[-2], refs[-1]
    width = whole.shape[1]
    channels = width // 3
    tail = channels % LANES
    body = channels - tail
    place_blocks(order, blocks, whole)
    spans = [(n * body, n * channels, body) for n in range(3)]
    if tail:
        spans += [(3 * body + n * tail, n * channels + body, tail) for n in range(3)]
    stores = []
    for i, (source, target, size) in enumerate(spans):
        turned[pl.ds(target, size), :] = whole[:, pl.ds(source, size)].T
        rows = pl.ds(target, size)
        stores.append(pltpu.make_async_copy(turned.at[rows], o_hbm.at[rows], sem.at[i]))
        stores[-1].start()
    for copy in stores:
        copy.wait()


def turn(order, staged, blocks):
    tokens, width = staged.shape
    return pl.pallas_call(
        functools.partial(turn_kernel, order),
        out_shape=(
            pltpu.VMEM((tokens, width), BF16),
            jax.ShapeDtypeStruct((width, tokens), BF16),
        ),
        in_specs=[pl.BlockSpec(memory_space=pltpu.VMEM)] * (1 + len(blocks)),
        out_specs=[pl.BlockSpec(memory_space=pltpu.VMEM), pl.BlockSpec(memory_space=pltpu.HBM)],
        scratch_shapes=[pltpu.VMEM((width, tokens), BF16), pltpu.SemaphoreType.DMA((6,))],
        input_output_aliases={0: 0},
        compiler_params=pltpu.CompilerParams(vmem_limit_bytes=24 << 20),
        name="turn",
    )(staged, *blocks)[1]


def partner_order(groups, inner):
    across = inner // 2

    def hops(s):
        return bin(s).count("1"), bin(s % inner).count("1"), s

    found = [across]
    for s in sorted((s for s in range(1, groups) if not s & across), key=hops):
        found += [s | across, s]
    return found


def local(cot, wos, wqkv, wot, qs, ks, vs, qt, kt, vt):
    tokens, features = cot.shape[1:]
    channels = qs.shape[2]
    axes = ("outer", "inner")
    groups = lax.axis_size(axes)
    pos_dev = tokens // groups
    inner = lax.axis_size("inner")
    direct = inner > 1 and groups <= 16 and groups & (groups - 1) == 0 and pos_dev % 8 == 0
    partners = [0] + partner_order(groups, inner) if direct else []

    middle, projected = spatial(
        cot[0], wos, wqkv.T, wot, qs[0].T, ks[0].T, vs[0].T
    )
    temporal_out = lax.all_to_all(
        projected.reshape(groups, pos_dev, channels), axes, split_axis=0, concat_axis=0, tiled=True
    )
    weights = probs(partners, qt, kt, direct)
    stacked = temporal(partners, qt, kt, vt, weights, temporal_out, direct)
    if direct:
        blocks = list(stacked)
        for n, s in enumerate(partners):
            if s:
                blocks[n] = lax.ppermute(stacked[n], axes, [(i, i ^ s) for i in range(groups)])
    else:
        returned = lax.all_to_all(stacked[0], axes, split_axis=0, concat_axis=0, tiled=True)
        blocks = [returned.reshape(tokens, 3 * channels)]
    late = len(blocks) * 5 // 16
    early = len(blocks) - late
    staged = stage(partners[:early], blocks[:early], tokens) if late else blocks[0]
    turned = turn(partners[early:], staged, blocks[early:])
    return (middle[None], turned.T[None])


def solution(mesh):
    frame = P(("sample", "outer", "inner"), None, None)
    place = P("sample", ("outer", "inner"), None)
    return jax.shard_map(
        local,
        mesh=mesh,
        in_specs=(frame, P(), P(), P(), frame, frame, frame, place, place, place),
        out_specs=(frame, frame),
        check_vma=False,
    )
```

```python
import functools
import math

import jax
import jax.numpy as jnp
from jax import lax
from jax.experimental import pallas as pl
from jax.experimental.pallas import tpu as pltpu
from jax.sharding import PartitionSpec as P

HEADS = 8
F32 = jnp.float32
BF16 = jnp.bfloat16
NN = (((1,), (0,)), ((), ()))
NT = (((1,), (1,)), ((), ()))
TN = (((0,), (0,)), ((), ()))
LANES = 128
LOG2E = math.log2(math.e)


def mm(a, b, dims):
    return lax.dot_general(a, b, dims, preferred_element_type=F32)


def pair_windows(channels, dim):
    found = []
    for h in range(0, HEADS, 2):
        low = h * dim // LANES * LANES
        high = min(channels, -(-(h + 2) * dim // LANES) * LANES)
        found.append((h, low, high))
    return found


def stack_pair(block, h, low, dim):
    lane = low + lax.broadcasted_iota(jnp.int32, block.shape, 1)
    zero = jnp.zeros_like(block)
    first = (lane >= h * dim) & (lane < (h + 1) * dim)
    second = (lane >= (h + 1) * dim) & (lane < (h + 2) * dim)
    return jnp.concatenate([jnp.where(first, block, zero), jnp.where(second, block, zero)], axis=0)


def softmax_rows(scores, exp_scale):
    top = jnp.max(scores, axis=0, keepdims=True)
    e = jnp.exp2((scores - top) * exp_scale)
    return e * (1.0 / jnp.sum(e, axis=0, keepdims=True))


def score_grad(p, grad_w):
    inner = jnp.sum(p * grad_w, axis=0, keepdims=True)
    return (p * (grad_w - inner)).astype(BF16)


def turn_halves(ds, rows):
    return jnp.concatenate([ds[:, :rows].T, ds[:, rows:].T], axis=1)


def add_tiles(tiles, window, low):
    for t in range(0, window.shape[1], LANES):
        piece = window[:, t : t + LANES]
        tiles[low + t] = tiles[low + t] + piece if low + t in tiles else piece


def spatial_kernel(
    cot_hbm, wos_hbm, wqkv_hbm, wot_hbm, q_hbm, k_hbm, v_hbm,
    mid_hbm, g,
    cot, wos, wqkv, wot, q, k, v, probs, sg, mid, sem,
):
    channels, tokens = q.shape
    dim = channels // HEADS
    scaling = dim ** (-0.5)
    exp_scale = scaling * LOG2E
    tail = channels % LANES
    body = channels - tail
    pairs = [(k_hbm, k), (q_hbm, q), (cot_hbm, cot), (wos_hbm, wos), (v_hbm, v)]
    for n in range(3):
        pairs.append((wqkv_hbm.at[pl.ds(n * channels, body)], wqkv.at[pl.ds(n * body, body)]))
    if tail:
        for n in range(3):
            pairs.append(
                (wqkv_hbm.at[pl.ds(n * channels + body, tail)], wqkv.at[pl.ds(3 * body + n * tail, tail)])
            )
    pairs.append((wot_hbm, wot))
    loads = [pltpu.make_async_copy(src, dst, sem.at[i]) for i, (src, dst) in enumerate(pairs)]
    for copy in loads:
        copy.start()
    windows = pair_windows(channels, dim)
    for copy in loads[:2]:
        copy.wait()
    k_n = k[...].T
    q_n = q[...].T

    def scores_of(n):
        h, low, high = windows[n]
        return mm(k_n[:, low:high], stack_pair(q_n[:, low:high], h, low, dim), NT)

    count = len(windows)
    scores = [scores_of(0), scores_of(1)]
    probs[0] = softmax_rows(scores[0], exp_scale)
    for copy in loads[2:5]:
        copy.wait()
    g_n = mm(cot[...], wos[...], NT).astype(BF16)
    probs[1] = softmax_rows(scores[1], exp_scale)
    v_n = v[...].T

    def grad_of(n):
        h, low, high = windows[n]
        stack = stack_pair(g_n[:, low:high], h, low, dim)
        return stack, mm(v_n[:, low:high], stack, NT)

    tiles = [{}, {}, {}]
    ahead = grad_of(0)
    for n, (h, low, high) in enumerate(windows):
        g_s, grad_w = ahead
        p = probs[n]
        if n + 1 < count:
            ahead = grad_of(n + 1)
        add_tiles(tiles[2], mm(p.astype(BF16), g_s, NN), low)
        if n + 2 < count:
            scores.append(scores_of(n + 2))
        ds = score_grad(p, grad_w)
        if n + 2 < count:
            probs[n + 2] = softmax_rows(scores[n + 2], exp_scale)
        add_tiles(tiles[1], mm(ds, stack_pair(q_n[:, low:high], h, low, dim), NN), low)
        add_tiles(tiles[0], mm(turn_halves(ds, tokens), stack_pair(k_n[:, low:high], h, low, dim), NN), low)
    for n in range(3):
        for t, tile in sorted(tiles[n].items()):
            if n < 2:
                tile = tile * scaling
            width = tile.shape[1]
            at = n * body + t if t < body else 3 * body + n * tail + t - body
            sg[:, at : at + width] = tile.astype(BF16)
    for copy in loads[5:-1]:
        copy.wait()
    middle = (cot[...].astype(F32) + mm(sg[...], wqkv[...], NN)).astype(BF16)
    mid[...] = middle
    out_mid = pltpu.make_async_copy(mid, mid_hbm, sem.at[len(loads)])
    out_mid.start()
    loads[-1].wait()
    g[...] = mm(middle, wot[...], NT).astype(BF16)
    out_mid.wait()


def spatial(cot, wos, wqkv_t, wot, q_t, k_t, v_t):
    channels, tokens = q_t.shape
    features = cot.shape[1]
    hbm_spec = pl.BlockSpec(memory_space=pltpu.HBM)
    ins = [cot, wos, wqkv_t, wot, q_t, k_t, v_t]
    ins = [pltpu.with_memory_space_constraint(a, pltpu.HBM) for a in ins]
    return pl.pallas_call(
        spatial_kernel,
        out_shape=(
            jax.ShapeDtypeStruct((tokens, features), BF16),
            pltpu.VMEM((tokens, channels), BF16),
        ),
        in_specs=[hbm_spec] * 7,
        out_specs=(hbm_spec, pl.BlockSpec(memory_space=pltpu.VMEM)),
        scratch_shapes=[pltpu.VMEM(a.shape, BF16) for a in ins]
        + [
            pltpu.VMEM((HEADS // 2, tokens, 2 * tokens), F32),
            pltpu.VMEM((tokens, 3 * channels), BF16),
            pltpu.VMEM((tokens, features), BF16),
            pltpu.SemaphoreType.DMA((13,)),
        ],
        compiler_params=pltpu.CompilerParams(vmem_limit_bytes=40 << 20),
        name="spatial",
    )(*ins)


def partner_of(s):
    return (lax.axis_index("outer") * lax.axis_size("inner") + lax.axis_index("inner")) ^ s


def frame_rows(ref, order, at, split):
    frames, _, channels = ref.shape
    if split:
        rows = [ref[partner_of(s), at, :].astype(F32) for s in order]
        block = jnp.concatenate(rows, axis=0)
    else:
        block = ref[:, at, :].astype(F32).reshape(-1, channels)
    return block.astype(BF16)


def probs_kernel(split, order, q_ref, k_ref, p_ref):
    frames, positions, channels = q_ref.shape
    dim = channels // HEADS
    exp_scale = dim ** (-0.5) * LOG2E
    step = math.gcd(positions, 8)
    rows = frames * step
    row = lax.broadcasted_iota(jnp.int32, (rows, 2 * rows), 0)
    col = lax.broadcasted_iota(jnp.int32, (rows, 2 * rows), 1)
    bias = jnp.where(lax.rem(row, step) == lax.rem(col, step), 0.0, -1e30).astype(F32)
    for j in range(positions // step):
        at = pl.ds(j * step, step)
        q, k = (frame_rows(a, order, at, split) for a in (q_ref, k_ref))
        for n, (h, low, high) in enumerate(pair_windows(channels, dim)):
            scores = mm(k[:, low:high], stack_pair(q[:, low:high], h, low, dim), NT)
            p_ref[j, n] = softmax_rows(scores + bias, exp_scale)


def probs(order, q, k, split):
    frames, positions, channels = q.shape
    step = math.gcd(positions, 8)
    rows = frames * step
    blocks = positions // step
    return pl.pallas_call(
        functools.partial(probs_kernel, split, order),
        out_shape=jax.ShapeDtypeStruct((blocks, HEADS // 2, rows, 2 * rows), F32),
        in_specs=[pl.BlockSpec(memory_space=pltpu.VMEM)] * 2,
        out_specs=pl.BlockSpec(memory_space=pltpu.VMEM),
        compiler_params=pltpu.CompilerParams(vmem_limit_bytes=24 << 20),
        cost_estimate=pl.CostEstimate(
            flops=blocks * HEADS * rows * rows * 1024,
            bytes_accessed=blocks * HEADS * rows * rows * 16,
            transcendentals=blocks * HEADS * rows * rows,
        ),
        name="probs",
    )(q, k)


def temporal_kernel(order, q_ref, k_ref, v_ref, p_ref, g_ref, *o_refs):
    frames, positions, channels = q_ref.shape
    dim = channels // HEADS
    scaling = dim ** (-0.5)
    step = math.gcd(positions, 8)
    rows = frames * step
    tail = channels % LANES
    split = len(o_refs) > 1
    windows = pair_windows(channels, dim)
    blocks = [pl.ds(j * step, step) for j in range(positions // step)]

    def begin(at):
        v, g = (frame_rows(a, order, at, split) for a in (v_ref, g_ref))
        stacks = [stack_pair(g[:, low:high], h, low, dim) for h, low, high in windows]
        return stacks, [mm(v[:, w[1] : w[2]], g_s, NT) for w, g_s in zip(windows, stacks)]

    begun = [begin(at) for at in blocks]
    for j, at in enumerate(blocks):
        g_stacks, grads = begun[j]
        q, k = (frame_rows(a, order, at, split) for a in (q_ref, k_ref))
        scores = [score_grad(p_ref[j, n], grad_w) for n, grad_w in enumerate(grads)]
        flipped = [turn_halves(ds, rows) for ds in scores]
        tiles = [{}, {}, {}]
        for n, (h, low, high) in enumerate(windows):
            q_s, k_s = (stack_pair(a[:, low:high], h, low, dim) for a in (q, k))
            add_tiles(tiles[2], mm(p_ref[j, n].astype(BF16), g_stacks[n], NN), low)
            add_tiles(tiles[1], mm(scores[n], q_s, NN), low)
            add_tiles(tiles[0], mm(flipped[n], k_s, NN), low)
        pieces, tails = [], []
        for n in range(3):
            part = [tile * scaling if n < 2 else tile for _, tile in sorted(tiles[n].items())]
            if tail:
                tails.append(part.pop())
            pieces += part
        whole = jnp.concatenate(pieces + tails, axis=1)
        if split:
            for s in range(frames):
                o_refs[s][at, :] = whole[s * step : (s + 1) * step].astype(BF16)
        else:
            o_refs[0][:, at, :] = whole.reshape(frames, step, 3 * channels).astype(BF16)


def temporal(order, q, k, v, p, g, split):
    frames, positions, channels = q.shape
    if split:
        shapes = [jax.ShapeDtypeStruct((positions, 3 * channels), BF16)] * frames
    else:
        shapes = [jax.ShapeDtypeStruct((frames, positions, 3 * channels), BF16)]
    return pl.pallas_call(
        functools.partial(temporal_kernel, order),
        out_shape=shapes,
        in_specs=[pl.BlockSpec(memory_space=pltpu.VMEM)] * 5,
        out_specs=[pl.BlockSpec(memory_space=pltpu.VMEM)] * len(shapes),
        compiler_params=pltpu.CompilerParams(vmem_limit_bytes=24 << 20),
        name="temporal",
    )(q, k, v, p, g)


def place_blocks(order, blocks, whole):
    for s, block in zip(order, blocks):
        each = block.shape[0]
        row = pl.multiple_of(partner_of(s) * each, 8)
        whole[pl.ds(row, each), :] = block[...]


def stage_kernel(order, *refs):
    place_blocks(order, refs[:-1], refs[-1])


def stage(order, blocks, tokens):
    width = blocks[0].shape[1]
    return pl.pallas_call(
        functools.partial(stage_kernel, order),
        out_shape=pltpu.VMEM((tokens, width), BF16),
        in_specs=[pl.BlockSpec(memory_space=pltpu.VMEM)] * len(blocks),
        out_specs=pl.BlockSpec(memory_space=pltpu.VMEM),
        compiler_params=pltpu.CompilerParams(vmem_limit_bytes=16 << 20),
        name="stage",
    )(*blocks)


def turn_kernel(order, staged, *refs):
    blocks, whole, o_hbm, turned, sem = refs[:-4], refs[-4], refs[-3], refs[-2], refs[-1]
    width = whole.shape[1]
    channels = width // 3
    tail = channels % LANES
    body = channels - tail
    place_blocks(order, blocks, whole)
    spans = [(n * body, n * channels, body) for n in range(3)]
    if tail:
        spans += [(3 * body + n * tail, n * channels + body, tail) for n in range(3)]
    stores = []
    for i, (source, target, size) in enumerate(spans):
        turned[pl.ds(target, size), :] = whole[:, pl.ds(source, size)].T
        rows = pl.ds(target, size)
        stores.append(pltpu.make_async_copy(turned.at[rows], o_hbm.at[rows], sem.at[i]))
        stores[-1].start()
    for copy in stores:
        copy.wait()


def turn(order, staged, blocks):
    tokens, width = staged.shape
    return pl.pallas_call(
        functools.partial(turn_kernel, order),
        out_shape=(
            pltpu.VMEM((tokens, width), BF16),
            jax.ShapeDtypeStruct((width, tokens), BF16),
        ),
        in_specs=[pl.BlockSpec(memory_space=pltpu.VMEM)] * (1 + len(blocks)),
        out_specs=[pl.BlockSpec(memory_space=pltpu.VMEM), pl.BlockSpec(memory_space=pltpu.HBM)],
        scratch_shapes=[pltpu.VMEM((width, tokens), BF16), pltpu.SemaphoreType.DMA((6,))],
        input_output_aliases={0: 0},
        compiler_params=pltpu.CompilerParams(vmem_limit_bytes=24 << 20),
        name="turn",
    )(staged, *blocks)[1]


def partner_order(groups, inner):
    across = inner // 2

    def hops(s):
        return bin(s).count("1"), bin(s % inner).count("1"), s

    found = [across]
    for s in sorted((s for s in range(1, groups) if not s & across), key=hops):
        found += [s | across, s]
    return found


def local(cot, wos, wqkv, wot, qs, ks, vs, qt, kt, vt):
    tokens, features = cot.shape[1:]
    channels = qs.shape[2]
    axes = ("outer", "inner")
    groups = lax.axis_size(axes)
    pos_dev = tokens // groups
    inner = lax.axis_size("inner")
    direct = inner > 1 and groups <= 16 and groups & (groups - 1) == 0 and pos_dev % 8 == 0
    partners = [0] + partner_order(groups, inner) if direct else []

    middle, projected = spatial(
        cot[0], wos, wqkv.T, wot, qs[0].T, ks[0].T, vs[0].T
    )
    temporal_out = lax.all_to_all(
        projected.reshape(groups, pos_dev, channels), axes, split_axis=0, concat_axis=0, tiled=True
    )
    weights = probs(partners, qt, kt, direct)
    stacked = temporal(partners, qt, kt, vt, weights, temporal_out, direct)
    if direct:
        blocks = list(stacked)
        for n, s in enumerate(partners):
            if s:
                blocks[n] = lax.ppermute(stacked[n], axes, [(i, i ^ s) for i in range(groups)])
    else:
        returned = lax.all_to_all(stacked[0], axes, split_axis=0, concat_axis=0, tiled=True)
        blocks = [returned.reshape(tokens, 3 * channels)]
    late = len(blocks) * 5 // 16
    early = len(blocks) - late
    staged = stage(partners[:early], blocks[:early], tokens) if late else blocks[0]
    turned = turn(partners[early:], staged, blocks[early:])
    return (middle[None], turned.T[None])


def solution(mesh):
    frame = P(("sample", "outer", "inner"), None, None)
    place = P("sample", ("outer", "inner"), None)
    return jax.shard_map(
        local,
        mesh=mesh,
        in_specs=(frame, P(), P(), P(), frame, frame, frame, place, place, place),
        out_specs=(frame, frame),
        check_vma=False,
    )
```

```python
import functools
import math

import jax
import jax.numpy as jnp
from jax import lax
from jax.experimental import pallas as pl
from jax.experimental.pallas import tpu as pltpu
from jax.sharding import PartitionSpec as P

HEADS = 8
F32 = jnp.float32
BF16 = jnp.bfloat16
NN = (((1,), (0,)), ((), ()))
NT = (((1,), (1,)), ((), ()))
TN = (((0,), (0,)), ((), ()))
LANES = 128
LOG2E = math.log2(math.e)


def mm(a, b, dims):
    return lax.dot_general(a, b, dims, preferred_element_type=F32)


def pair_windows(channels, dim):
    found = []
    for h in range(0, HEADS, 2):
        low = h * dim // LANES * LANES
        high = min(channels, -(-(h + 2) * dim // LANES) * LANES)
        found.append((h, low, high))
    return found


def stack_pair(block, h, low, dim):
    lane = low + lax.broadcasted_iota(jnp.int32, block.shape, 1)
    zero = jnp.zeros_like(block)
    first = (lane >= h * dim) & (lane < (h + 1) * dim)
    second = (lane >= (h + 1) * dim) & (lane < (h + 2) * dim)
    return jnp.concatenate([jnp.where(first, block, zero), jnp.where(second, block, zero)], axis=0)


def softmax_rows(scores, exp_scale):
    top = jnp.max(scores, axis=0, keepdims=True)
    e = jnp.exp2((scores - top) * exp_scale)
    return e * (1.0 / jnp.sum(e, axis=0, keepdims=True))


def score_grad(p, grad_w):
    inner = jnp.sum(p * grad_w, axis=0, keepdims=True)
    return (p * (grad_w - inner)).astype(BF16)


def turn_halves(ds, rows):
    return jnp.concatenate([ds[:, :rows].T, ds[:, rows:].T], axis=1)


def add_tiles(tiles, window, low):
    for t in range(0, window.shape[1], LANES):
        piece = window[:, t : t + LANES]
        tiles[low + t] = tiles[low + t] + piece if low + t in tiles else piece


def spatial_kernel(
    cot_hbm, wos_hbm, wqkv_hbm, wot_hbm, q_hbm, k_hbm, v_hbm,
    mid_hbm, g,
    cot, wos, wqkv, wot, q, k, v, probs, sg, mid, sem,
):
    channels, tokens = q.shape
    dim = channels // HEADS
    scaling = dim ** (-0.5)
    exp_scale = scaling * LOG2E
    tail = channels % LANES
    body = channels - tail
    pairs = [(k_hbm, k), (q_hbm, q), (cot_hbm, cot), (wos_hbm, wos), (v_hbm, v)]
    for n in range(3):
        pairs.append((wqkv_hbm.at[pl.ds(n * channels, body)], wqkv.at[pl.ds(n * body, body)]))
    if tail:
        for n in range(3):
            pairs.append(
                (wqkv_hbm.at[pl.ds(n * channels + body, tail)], wqkv.at[pl.ds(3 * body + n * tail, tail)])
            )
    pairs.append((wot_hbm, wot))
    loads = [pltpu.make_async_copy(src, dst, sem.at[i]) for i, (src, dst) in enumerate(pairs)]
    for copy in loads:
        copy.start()
    windows = pair_windows(channels, dim)
    for copy in loads[:2]:
        copy.wait()
    k_n = k[...].T
    q_n = q[...].T

    def scores_of(n):
        h, low, high = windows[n]
        return mm(k_n[:, low:high], stack_pair(q_n[:, low:high], h, low, dim), NT)

    count = len(windows)
    scores = [scores_of(0), scores_of(1)]
    probs[0] = softmax_rows(scores[0], exp_scale)
    for copy in loads[2:5]:
        copy.wait()
    g_n = mm(cot[...], wos[...], NT).astype(BF16)
    probs[1] = softmax_rows(scores[1], exp_scale)
    v_n = v[...].T

    def grad_of(n):
        h, low, high = windows[n]
        stack = stack_pair(g_n[:, low:high], h, low, dim)
        return stack, mm(v_n[:, low:high], stack, NT)

    tiles = [{}, {}, {}]
    ahead = grad_of(0)
    for n, (h, low, high) in enumerate(windows):
        g_s, grad_w = ahead
        p = probs[n]
        if n + 1 < count:
            ahead = grad_of(n + 1)
        add_tiles(tiles[2], mm(p.astype(BF16), g_s, NN), low)
        if n + 2 < count:
            scores.append(scores_of(n + 2))
        ds = score_grad(p, grad_w)
        if n + 2 < count:
            probs[n + 2] = softmax_rows(scores[n + 2], exp_scale)
        add_tiles(tiles[1], mm(ds, stack_pair(q_n[:, low:high], h, low, dim), NN), low)
        add_tiles(tiles[0], mm(turn_halves(ds, tokens), stack_pair(k_n[:, low:high], h, low, dim), NN), low)
    for n in range(3):
        for t, tile in sorted(tiles[n].items()):
            if n < 2:
                tile = tile * scaling
            width = tile.shape[1]
            at = n * body + t if t < body else 3 * body + n * tail + t - body
            sg[:, at : at + width] = tile.astype(BF16)
    for copy in loads[5:-1]:
        copy.wait()
    middle = (cot[...].astype(F32) + mm(sg[...], wqkv[...], NN)).astype(BF16)
    mid[...] = middle
    out_mid = pltpu.make_async_copy(mid, mid_hbm, sem.at[len(loads)])
    out_mid.start()
    loads[-1].wait()
    g[...] = mm(middle, wot[...], NT).astype(BF16)
    out_mid.wait()


def spatial(cot, wos, wqkv_t, wot, q_t, k_t, v_t):
    channels, tokens = q_t.shape
    features = cot.shape[1]
    hbm_spec = pl.BlockSpec(memory_space=pltpu.HBM)
    ins = [cot, wos, wqkv_t, wot, q_t, k_t, v_t]
    ins = [pltpu.with_memory_space_constraint(a, pltpu.HBM) for a in ins]
    return pl.pallas_call(
        spatial_kernel,
        out_shape=(
            jax.ShapeDtypeStruct((tokens, features), BF16),
            pltpu.VMEM((tokens, channels), BF16),
        ),
        in_specs=[hbm_spec] * 7,
        out_specs=(hbm_spec, pl.BlockSpec(memory_space=pltpu.VMEM)),
        scratch_shapes=[pltpu.VMEM(a.shape, BF16) for a in ins]
        + [
            pltpu.VMEM((HEADS // 2, tokens, 2 * tokens), F32),
            pltpu.VMEM((tokens, 3 * channels), BF16),
            pltpu.VMEM((tokens, features), BF16),
            pltpu.SemaphoreType.DMA((13,)),
        ],
        compiler_params=pltpu.CompilerParams(vmem_limit_bytes=40 << 20),
        name="spatial",
    )(*ins)


def partner_of(s):
    return (lax.axis_index("outer") * lax.axis_size("inner") + lax.axis_index("inner")) ^ s


def frame_rows(ref, order, at, split):
    frames, _, channels = ref.shape
    if split:
        rows = [ref[partner_of(s), at, :].astype(F32) for s in order]
        block = jnp.concatenate(rows, axis=0)
    else:
        block = ref[:, at, :].astype(F32).reshape(-1, channels)
    return block.astype(BF16)


def probs_kernel(split, order, q_ref, k_ref, p_ref):
    frames, positions, channels = q_ref.shape
    dim = channels // HEADS
    exp_scale = dim ** (-0.5) * LOG2E
    step = math.gcd(positions, 8)
    rows = frames * step
    row = lax.broadcasted_iota(jnp.int32, (rows, 2 * rows), 0)
    col = lax.broadcasted_iota(jnp.int32, (rows, 2 * rows), 1)
    bias = jnp.where(lax.rem(row, step) == lax.rem(col, step), 0.0, -1e30).astype(F32)
    for j in range(positions // step):
        at = pl.ds(j * step, step)
        q, k = (frame_rows(a, order, at, split) for a in (q_ref, k_ref))
        for n, (h, low, high) in enumerate(pair_windows(channels, dim)):
            scores = mm(k[:, low:high], stack_pair(q[:, low:high], h, low, dim), NT)
            p_ref[j, n] = softmax_rows(scores + bias, exp_scale)


def probs(order, q, k, split):
    frames, positions, channels = q.shape
    step = math.gcd(positions, 8)
    rows = frames * step
    blocks = positions // step
    return pl.pallas_call(
        functools.partial(probs_kernel, split, order),
        out_shape=jax.ShapeDtypeStruct((blocks, HEADS // 2, rows, 2 * rows), F32),
        in_specs=[pl.BlockSpec(memory_space=pltpu.VMEM)] * 2,
        out_specs=pl.BlockSpec(memory_space=pltpu.VMEM),
        compiler_params=pltpu.CompilerParams(vmem_limit_bytes=24 << 20),
        cost_estimate=pl.CostEstimate(
            flops=blocks * HEADS * rows * rows * 1024,
            bytes_accessed=blocks * HEADS * rows * rows * 16,
            transcendentals=blocks * HEADS * rows * rows,
        ),
        name="probs",
    )(q, k)


def temporal_kernel(order, q_ref, k_ref, v_ref, p_ref, g_ref, *o_refs):
    frames, positions, channels = q_ref.shape
    dim = channels // HEADS
    scaling = dim ** (-0.5)
    step = math.gcd(positions, 8)
    rows = frames * step
    tail = channels % LANES
    split = len(o_refs) > 1
    windows = pair_windows(channels, dim)
    blocks = [pl.ds(j * step, step) for j in range(positions // step)]

    def begin(at):
        v, g = (frame_rows(a, order, at, split) for a in (v_ref, g_ref))
        stacks = [stack_pair(g[:, low:high], h, low, dim) for h, low, high in windows]
        return stacks, [mm(v[:, w[1] : w[2]], g_s, NT) for w, g_s in zip(windows, stacks)]

    begun = [begin(at) for at in blocks]
    for j, at in enumerate(blocks):
        g_stacks, grads = begun[j]
        q, k = (frame_rows(a, order, at, split) for a in (q_ref, k_ref))
        scores = [score_grad(p_ref[j, n], grad_w) for n, grad_w in enumerate(grads)]
        flipped = [turn_halves(ds, rows) for ds in scores]
        tiles = [{}, {}, {}]
        for n, (h, low, high) in enumerate(windows):
            q_s, k_s = (stack_pair(a[:, low:high], h, low, dim) for a in (q, k))
            add_tiles(tiles[2], mm(p_ref[j, n].astype(BF16), g_stacks[n], NN), low)
            add_tiles(tiles[1], mm(scores[n], q_s, NN), low)
            add_tiles(tiles[0], mm(flipped[n], k_s, NN), low)
        pieces, tails = [], []
        for n in range(3):
            part = [tile * scaling if n < 2 else tile for _, tile in sorted(tiles[n].items())]
            if tail:
                tails.append(part.pop())
            pieces += part
        whole = jnp.concatenate(pieces + tails, axis=1)
        if split:
            for s in range(frames):
                o_refs[s][at, :] = whole[s * step : (s + 1) * step].astype(BF16)
        else:
            o_refs[0][:, at, :] = whole.reshape(frames, step, 3 * channels).astype(BF16)


def temporal(order, q, k, v, p, g, split):
    frames, positions, channels = q.shape
    if split:
        shapes = [jax.ShapeDtypeStruct((positions, 3 * channels), BF16)] * frames
    else:
        shapes = [jax.ShapeDtypeStruct((frames, positions, 3 * channels), BF16)]
    return pl.pallas_call(
        functools.partial(temporal_kernel, order),
        out_shape=shapes,
        in_specs=[pl.BlockSpec(memory_space=pltpu.VMEM)] * 5,
        out_specs=[pl.BlockSpec(memory_space=pltpu.VMEM)] * len(shapes),
        compiler_params=pltpu.CompilerParams(vmem_limit_bytes=24 << 20),
        name="temporal",
    )(q, k, v, p, g)


def place_blocks(order, blocks, whole):
    for s, block in zip(order, blocks):
        each = block.shape[0]
        row = pl.multiple_of(partner_of(s) * each, 8)
        whole[pl.ds(row, each), :] = block[...]


def stage_kernel(order, *refs):
    place_blocks(order, refs[:-1], refs[-1])


def stage(order, blocks, tokens):
    width = blocks[0].shape[1]
    return pl.pallas_call(
        functools.partial(stage_kernel, order),
        out_shape=pltpu.VMEM((tokens, width), BF16),
        in_specs=[pl.BlockSpec(memory_space=pltpu.VMEM)] * len(blocks),
        out_specs=pl.BlockSpec(memory_space=pltpu.VMEM),
        compiler_params=pltpu.CompilerParams(vmem_limit_bytes=16 << 20),
        name="stage",
    )(*blocks)


def turn_kernel(order, staged, *refs):
    blocks, whole, o_hbm, turned, sem = refs[:-4], refs[-4], refs[-3], refs[-2], refs[-1]
    width = whole.shape[1]
    channels = width // 3
    tail = channels % LANES
    body = channels - tail
    place_blocks(order, blocks, whole)
    spans = [(n * body, n * channels, body) for n in range(3)]
    if tail:
        spans += [(3 * body + n * tail, n * channels + body, tail) for n in range(3)]
    stores = []
    for i, (source, target, size) in enumerate(spans):
        turned[pl.ds(target, size), :] = whole[:, pl.ds(source, size)].T
        rows = pl.ds(target, size)
        stores.append(pltpu.make_async_copy(turned.at[rows], o_hbm.at[rows], sem.at[i]))
        stores[-1].start()
    for copy in stores:
        copy.wait()


def turn(order, staged, blocks):
    tokens, width = staged.shape
    return pl.pallas_call(
        functools.partial(turn_kernel, order),
        out_shape=(
            pltpu.VMEM((tokens, width), BF16),
            jax.ShapeDtypeStruct((width, tokens), BF16),
        ),
        in_specs=[pl.BlockSpec(memory_space=pltpu.VMEM)] * (1 + len(blocks)),
        out_specs=[pl.BlockSpec(memory_space=pltpu.VMEM), pl.BlockSpec(memory_space=pltpu.HBM)],
        scratch_shapes=[pltpu.VMEM((width, tokens), BF16), pltpu.SemaphoreType.DMA((6,))],
        input_output_aliases={0: 0},
        compiler_params=pltpu.CompilerParams(vmem_limit_bytes=24 << 20),
        name="turn",
    )(staged, *blocks)[1]


def partner_order(groups, inner):
    across = inner // 2

    def hops(s):
        return bin(s).count("1"), bin(s % inner).count("1"), s

    found = [across]
    for s in sorted((s for s in range(1, groups) if not s & across), key=hops):
        found += [s | across, s]
    return found


def local(cot, wos, wqkv, wot, qs, ks, vs, qt, kt, vt):
    tokens, features = cot.shape[1:]
    channels = qs.shape[2]
    axes = ("outer", "inner")
    groups = lax.axis_size(axes)
    pos_dev = tokens // groups
    inner = lax.axis_size("inner")
    direct = inner > 1 and groups <= 16 and groups & (groups - 1) == 0 and pos_dev % 8 == 0
    partners = [0] + partner_order(groups, inner) if direct else []

    middle, projected = spatial(
        cot[0], wos, wqkv.T, wot, qs[0].T, ks[0].T, vs[0].T
    )
    temporal_out = lax.all_to_all(
        projected.reshape(groups, pos_dev, channels), axes, split_axis=0, concat_axis=0, tiled=True
    )
    weights = probs(partners, qt, kt, direct)
    stacked = temporal(partners, qt, kt, vt, weights, temporal_out, direct)
    if direct:
        blocks = list(stacked)
        for n, s in enumerate(partners):
            if s:
                blocks[n] = lax.ppermute(stacked[n], axes, [(i, i ^ s) for i in range(groups)])
    else:
        returned = lax.all_to_all(stacked[0], axes, split_axis=0, concat_axis=0, tiled=True)
        blocks = [returned.reshape(tokens, 3 * channels)]
    late = len(blocks) * 3 // 16
    early = len(blocks) - late
    staged = stage(partners[:early], blocks[:early], tokens) if late else blocks[0]
    turned = turn(partners[early:], staged, blocks[early:])
    return (middle[None], turned.T[None])


def solution(mesh):
    frame = P(("sample", "outer", "inner"), None, None)
    place = P("sample", ("outer", "inner"), None)
    return jax.shard_map(
        local,
        mesh=mesh,
        in_specs=(frame, P(), P(), P(), frame, frame, frame, place, place, place),
        out_specs=(frame, frame),
        check_vma=False,
    )
```

```python
import functools
import math

import jax
import jax.numpy as jnp
from jax import lax
from jax.experimental import pallas as pl
from jax.experimental.pallas import tpu as pltpu
from jax.sharding import PartitionSpec as P

HEADS = 8
F32 = jnp.float32
BF16 = jnp.bfloat16
NN = (((1,), (0,)), ((), ()))
NT = (((1,), (1,)), ((), ()))
TN = (((0,), (0,)), ((), ()))
LANES = 128
LOG2E = math.log2(math.e)


def mm(a, b, dims):
    return lax.dot_general(a, b, dims, preferred_element_type=F32)


def pair_windows(channels, dim):
    found = []
    for h in range(0, HEADS, 2):
        low = h * dim // LANES * LANES
        high = min(channels, -(-(h + 2) * dim // LANES) * LANES)
        found.append((h, low, high))
    return found


def stack_pair(block, h, low, dim):
    lane = low + lax.broadcasted_iota(jnp.int32, block.shape, 1)
    zero = jnp.zeros_like(block)
    first = (lane >= h * dim) & (lane < (h + 1) * dim)
    second = (lane >= (h + 1) * dim) & (lane < (h + 2) * dim)
    return jnp.concatenate([jnp.where(first, block, zero), jnp.where(second, block, zero)], axis=0)


def softmax_rows(scores, exp_scale):
    top = jnp.max(scores, axis=0, keepdims=True)
    e = jnp.exp2((scores - top) * exp_scale)
    return e * (1.0 / jnp.sum(e, axis=0, keepdims=True))


def score_grad(p, grad_w):
    inner = jnp.sum(p * grad_w, axis=0, keepdims=True)
    return (p * (grad_w - inner)).astype(BF16)


def turn_halves(ds, rows):
    return jnp.concatenate([ds[:, :rows].T, ds[:, rows:].T], axis=1)


def add_tiles(tiles, window, low):
    for t in range(0, window.shape[1], LANES):
        piece = window[:, t : t + LANES]
        tiles[low + t] = tiles[low + t] + piece if low + t in tiles else piece


def spatial_kernel(
    cot_hbm, wos_hbm, wqkv_hbm, wot_hbm, q_hbm, k_hbm, v_hbm,
    mid_hbm, g,
    cot, wos, wqkv, wot, q, k, v, probs, sg, mid, sem,
):
    channels, tokens = q.shape
    dim = channels // HEADS
    scaling = dim ** (-0.5)
    exp_scale = scaling * LOG2E
    tail = channels % LANES
    body = channels - tail
    pairs = [(k_hbm, k), (q_hbm, q), (wos_hbm, wos), (cot_hbm, cot), (v_hbm, v)]
    for n in range(3):
        pairs.append((wqkv_hbm.at[pl.ds(n * channels, body)], wqkv.at[pl.ds(n * body, body)]))
    if tail:
        for n in range(3):
            pairs.append(
                (wqkv_hbm.at[pl.ds(n * channels + body, tail)], wqkv.at[pl.ds(3 * body + n * tail, tail)])
            )
    pairs.append((wot_hbm, wot))
    loads = [pltpu.make_async_copy(src, dst, sem.at[i]) for i, (src, dst) in enumerate(pairs)]
    for copy in loads:
        copy.start()
    windows = pair_windows(channels, dim)
    for copy in loads[:2]:
        copy.wait()
    k_n = k[...].T
    q_n = q[...].T

    def scores_of(n):
        h, low, high = windows[n]
        return mm(k_n[:, low:high], stack_pair(q_n[:, low:high], h, low, dim), NT)

    count = len(windows)
    scores = [scores_of(0), scores_of(1)]
    probs[0] = softmax_rows(scores[0], exp_scale)
    for copy in loads[2:5]:
        copy.wait()
    g_n = mm(cot[...], wos[...], NT).astype(BF16)
    probs[1] = softmax_rows(scores[1], exp_scale)
    v_n = v[...].T

    def grad_of(n):
        h, low, high = windows[n]
        stack = stack_pair(g_n[:, low:high], h, low, dim)
        return stack, mm(v_n[:, low:high], stack, NT)

    tiles = [{}, {}, {}]
    ahead = grad_of(0)
    for n, (h, low, high) in enumerate(windows):
        g_s, grad_w = ahead
        p = probs[n]
        if n + 1 < count:
            ahead = grad_of(n + 1)
        add_tiles(tiles[2], mm(p.astype(BF16), g_s, NN), low)
        if n + 2 < count:
            scores.append(scores_of(n + 2))
        ds = score_grad(p, grad_w)
        if n + 2 < count:
            probs[n + 2] = softmax_rows(scores[n + 2], exp_scale)
        add_tiles(tiles[1], mm(ds, stack_pair(q_n[:, low:high], h, low, dim), NN), low)
        add_tiles(tiles[0], mm(turn_halves(ds, tokens), stack_pair(k_n[:, low:high], h, low, dim), NN), low)
    for n in range(3):
        for t, tile in sorted(tiles[n].items()):
            if n < 2:
                tile = tile * scaling
            width = tile.shape[1]
            at = n * body + t if t < body else 3 * body + n * tail + t - body
            sg[:, at : at + width] = tile.astype(BF16)
    for copy in loads[5:-1]:
        copy.wait()
    middle = (cot[...].astype(F32) + mm(sg[...], wqkv[...], NN)).astype(BF16)
    mid[...] = middle
    out_mid = pltpu.make_async_copy(mid, mid_hbm, sem.at[len(loads)])
    out_mid.start()
    loads[-1].wait()
    g[...] = mm(middle, wot[...], NT).astype(BF16)
    out_mid.wait()


def spatial(cot, wos, wqkv_t, wot, q_t, k_t, v_t):
    channels, tokens = q_t.shape
    features = cot.shape[1]
    hbm_spec = pl.BlockSpec(memory_space=pltpu.HBM)
    ins = [cot, wos, wqkv_t, wot, q_t, k_t, v_t]
    ins = [pltpu.with_memory_space_constraint(a, pltpu.HBM) for a in ins]
    return pl.pallas_call(
        spatial_kernel,
        out_shape=(
            jax.ShapeDtypeStruct((tokens, features), BF16),
            pltpu.VMEM((tokens, channels), BF16),
        ),
        in_specs=[hbm_spec] * 7,
        out_specs=(hbm_spec, pl.BlockSpec(memory_space=pltpu.VMEM)),
        scratch_shapes=[pltpu.VMEM(a.shape, BF16) for a in ins]
        + [
            pltpu.VMEM((HEADS // 2, tokens, 2 * tokens), F32),
            pltpu.VMEM((tokens, 3 * channels), BF16),
            pltpu.VMEM((tokens, features), BF16),
            pltpu.SemaphoreType.DMA((13,)),
        ],
        compiler_params=pltpu.CompilerParams(vmem_limit_bytes=40 << 20),
        name="spatial",
    )(*ins)


def partner_of(s):
    return (lax.axis_index("outer") * lax.axis_size("inner") + lax.axis_index("inner")) ^ s


def frame_rows(ref, order, at, split):
    frames, _, channels = ref.shape
    if split:
        rows = [ref[partner_of(s), at, :].astype(F32) for s in order]
        block = jnp.concatenate(rows, axis=0)
    else:
        block = ref[:, at, :].astype(F32).reshape(-1, channels)
    return block.astype(BF16)


def probs_kernel(split, order, q_ref, k_ref, p_ref):
    frames, positions, channels = q_ref.shape
    dim = channels // HEADS
    exp_scale = dim ** (-0.5) * LOG2E
    step = math.gcd(positions, 8)
    rows = frames * step
    row = lax.broadcasted_iota(jnp.int32, (rows, 2 * rows), 0)
    col = lax.broadcasted_iota(jnp.int32, (rows, 2 * rows), 1)
    bias = jnp.where(lax.rem(row, step) == lax.rem(col, step), 0.0, -1e30).astype(F32)
    for j in range(positions // step):
        at = pl.ds(j * step, step)
        q, k = (frame_rows(a, order, at, split) for a in (q_ref, k_ref))
        for n, (h, low, high) in enumerate(pair_windows(channels, dim)):
            scores = mm(k[:, low:high], stack_pair(q[:, low:high], h, low, dim), NT)
            p_ref[j, n] = softmax_rows(scores + bias, exp_scale)


def probs(order, q, k, split):
    frames, positions, channels = q.shape
    step = math.gcd(positions, 8)
    rows = frames * step
    blocks = positions // step
    return pl.pallas_call(
        functools.partial(probs_kernel, split, order),
        out_shape=jax.ShapeDtypeStruct((blocks, HEADS // 2, rows, 2 * rows), F32),
        in_specs=[pl.BlockSpec(memory_space=pltpu.VMEM)] * 2,
        out_specs=pl.BlockSpec(memory_space=pltpu.VMEM),
        compiler_params=pltpu.CompilerParams(vmem_limit_bytes=24 << 20),
        cost_estimate=pl.CostEstimate(
            flops=blocks * HEADS * rows * rows * 1024,
            bytes_accessed=blocks * HEADS * rows * rows * 16,
            transcendentals=blocks * HEADS * rows * rows,
        ),
        name="probs",
    )(q, k)


def temporal_kernel(order, q_ref, k_ref, v_ref, p_ref, g_ref, *o_refs):
    frames, positions, channels = q_ref.shape
    dim = channels // HEADS
    scaling = dim ** (-0.5)
    step = math.gcd(positions, 8)
    rows = frames * step
    tail = channels % LANES
    split = len(o_refs) > 1
    windows = pair_windows(channels, dim)
    blocks = [pl.ds(j * step, step) for j in range(positions // step)]

    def begin(at):
        v, g = (frame_rows(a, order, at, split) for a in (v_ref, g_ref))
        stacks = [stack_pair(g[:, low:high], h, low, dim) for h, low, high in windows]
        return stacks, [mm(v[:, w[1] : w[2]], g_s, NT) for w, g_s in zip(windows, stacks)]

    begun = [begin(at) for at in blocks]
    for j, at in enumerate(blocks):
        g_stacks, grads = begun[j]
        q, k = (frame_rows(a, order, at, split) for a in (q_ref, k_ref))
        scores = [score_grad(p_ref[j, n], grad_w) for n, grad_w in enumerate(grads)]
        flipped = [turn_halves(ds, rows) for ds in scores]
        tiles = [{}, {}, {}]
        for n, (h, low, high) in enumerate(windows):
            q_s, k_s = (stack_pair(a[:, low:high], h, low, dim) for a in (q, k))
            add_tiles(tiles[2], mm(p_ref[j, n].astype(BF16), g_stacks[n], NN), low)
            add_tiles(tiles[1], mm(scores[n], q_s, NN), low)
            add_tiles(tiles[0], mm(flipped[n], k_s, NN), low)
        pieces, tails = [], []
        for n in range(3):
            part = [tile * scaling if n < 2 else tile for _, tile in sorted(tiles[n].items())]
            if tail:
                tails.append(part.pop())
            pieces += part
        whole = jnp.concatenate(pieces + tails, axis=1)
        if split:
            for s in range(frames):
                o_refs[s][at, :] = whole[s * step : (s + 1) * step].astype(BF16)
        else:
            o_refs[0][:, at, :] = whole.reshape(frames, step, 3 * channels).astype(BF16)


def temporal(order, q, k, v, p, g, split):
    frames, positions, channels = q.shape
    if split:
        shapes = [jax.ShapeDtypeStruct((positions, 3 * channels), BF16)] * frames
    else:
        shapes = [jax.ShapeDtypeStruct((frames, positions, 3 * channels), BF16)]
    return pl.pallas_call(
        functools.partial(temporal_kernel, order),
        out_shape=shapes,
        in_specs=[pl.BlockSpec(memory_space=pltpu.VMEM)] * 5,
        out_specs=[pl.BlockSpec(memory_space=pltpu.VMEM)] * len(shapes),
        compiler_params=pltpu.CompilerParams(vmem_limit_bytes=24 << 20),
        name="temporal",
    )(q, k, v, p, g)


def place_blocks(order, blocks, whole):
    for s, block in zip(order, blocks):
        each = block.shape[0]
        row = pl.multiple_of(partner_of(s) * each, 8)
        whole[pl.ds(row, each), :] = block[...]


def stage_kernel(order, *refs):
    place_blocks(order, refs[:-1], refs[-1])


def stage(order, blocks, tokens):
    width = blocks[0].shape[1]
    return pl.pallas_call(
        functools.partial(stage_kernel, order),
        out_shape=pltpu.VMEM((tokens, width), BF16),
        in_specs=[pl.BlockSpec(memory_space=pltpu.VMEM)] * len(blocks),
        out_specs=pl.BlockSpec(memory_space=pltpu.VMEM),
        compiler_params=pltpu.CompilerParams(vmem_limit_bytes=16 << 20),
        name="stage",
    )(*blocks)


def turn_kernel(order, staged, *refs):
    blocks, whole, o_hbm, turned, sem = refs[:-4], refs[-4], refs[-3], refs[-2], refs[-1]
    width = whole.shape[1]
    channels = width // 3
    tail = channels % LANES
    body = channels - tail
    place_blocks(order, blocks, whole)
    spans = [(n * body, n * channels, body) for n in range(3)]
    if tail:
        spans += [(3 * body + n * tail, n * channels + body, tail) for n in range(3)]
    stores = []
    for i, (source, target, size) in enumerate(spans):
        turned[pl.ds(target, size), :] = whole[:, pl.ds(source, size)].T
        rows = pl.ds(target, size)
        stores.append(pltpu.make_async_copy(turned.at[rows], o_hbm.at[rows], sem.at[i]))
        stores[-1].start()
    for copy in stores:
        copy.wait()


def turn(order, staged, blocks):
    tokens, width = staged.shape
    return pl.pallas_call(
        functools.partial(turn_kernel, order),
        out_shape=(
            pltpu.VMEM((tokens, width), BF16),
            jax.ShapeDtypeStruct((width, tokens), BF16),
        ),
        in_specs=[pl.BlockSpec(memory_space=pltpu.VMEM)] * (1 + len(blocks)),
        out_specs=[pl.BlockSpec(memory_space=pltpu.VMEM), pl.BlockSpec(memory_space=pltpu.HBM)],
        scratch_shapes=[pltpu.VMEM((width, tokens), BF16), pltpu.SemaphoreType.DMA((6,))],
        input_output_aliases={0: 0},
        compiler_params=pltpu.CompilerParams(vmem_limit_bytes=24 << 20),
        name="turn",
    )(staged, *blocks)[1]


def partner_order(groups, inner):
    across = inner // 2

    def hops(s):
        return bin(s).count("1"), bin(s % inner).count("1"), s

    found = [across]
    for s in sorted((s for s in range(1, groups) if not s & across), key=hops):
        found += [s | across, s]
    return found


def local(cot, wos, wqkv, wot, qs, ks, vs, qt, kt, vt):
    tokens, features = cot.shape[1:]
    channels = qs.shape[2]
    axes = ("outer", "inner")
    groups = lax.axis_size(axes)
    pos_dev = tokens // groups
    inner = lax.axis_size("inner")
    direct = inner > 1 and groups <= 16 and groups & (groups - 1) == 0 and pos_dev % 8 == 0
    partners = [0] + partner_order(groups, inner) if direct else []

    middle, projected = spatial(
        cot[0], wos, wqkv.T, wot, qs[0].T, ks[0].T, vs[0].T
    )
    temporal_out = lax.all_to_all(
        projected.reshape(groups, pos_dev, channels), axes, split_axis=0, concat_axis=0, tiled=True
    )
    weights = probs(partners, qt, kt, direct)
    stacked = temporal(partners, qt, kt, vt, weights, temporal_out, direct)
    if direct:
        blocks = list(stacked)
        for n, s in enumerate(partners):
            if s:
                blocks[n] = lax.ppermute(stacked[n], axes, [(i, i ^ s) for i in range(groups)])
    else:
        returned = lax.all_to_all(stacked[0], axes, split_axis=0, concat_axis=0, tiled=True)
        blocks = [returned.reshape(tokens, 3 * channels)]
    late = len(blocks) * 5 // 16
    early = len(blocks) - late
    staged = stage(partners[:early], blocks[:early], tokens) if late else blocks[0]
    turned = turn(partners[early:], staged, blocks[early:])
    return (middle[None], turned.T[None])


def solution(mesh):
    frame = P(("sample", "outer", "inner"), None, None)
    place = P("sample", ("outer", "inner"), None)
    return jax.shard_map(
        local,
        mesh=mesh,
        in_specs=(frame, P(), P(), P(), frame, frame, frame, place, place, place),
        out_specs=(frame, frame),
        check_vma=False,
    )
```
